32 devices in a mesh: dp: 8 (over y, x, core), space: 4 (over z).
Axes of the slice: x: 2, y: 2, z: 4, core: 2. Of those that a mesh axis runs over, the one named last changes fastest.
Arguments:
- features: bfloat16 [8, 32, 16, 512], P('dp', 'space'), may hold values from -48 to 48
- cotangent: bfloat16 [8, 32, 16, 512], P('dp', 'space'), may hold values from -6 to 6
- dw_kernel: float32 [7, 7, 512], replicated, may hold values from -0.875 to 0.875
- ln_gain: float32 [512], replicated, may hold values from 0.1 to 1.9
- ln_bias: float32 [512], replicated, may hold values from -3 to 3
- layer_scale: float32 [512], replicated, may hold values from 0.3 to 3
- w_up: bfloat16 [512, 2048], P('dp'), may hold values from -0.25 to 0.25
- w_down: bfloat16 [2048, 512], P('dp'), may hold values from -0.125 to 0.125
Outputs:
- result: bfloat16 [8, 32, 16, 512], P('dp', 'space')
- d_features: float32 [8, 32, 16, 512], P('dp', 'space')
- d_w_up: float32 [512, 2048], P('dp', 'space')
- d_w_down: float32 [2048, 512], P('space', 'dp')
- d_kernel: float32 [7, 7, 512], replicated
- d_gain: float32 [512], replicated
- d_bias: float32 [512], replicated
- d_scale: float32 [512], replicated
The draws below stay inside these ranges and needn't reach their ends.
All inputs are finite; a program needn't handle non-finite values.
Results may differ from the reference program's by a relative error of at most 0.0065.
Values may be sent and summed in bfloat16 or wider, within the bound.
A program may use at most 64 MiB of HBM per device.

```python
import math
import jax
import jax.numpy as jnp
from jax import lax

D = 512
FF = 2048
KW = 7
COLS = 16
REGIONS = 8
REGION_ROWS = 32
N_DP = 8


def draw_features(key, part):
    base_key, chan_key, pixel_key = jax.random.split(key, 3)
    shape = (REGIONS, REGION_ROWS, COLS, D)
    channel_scale = jnp.exp(jax.random.uniform(chan_key, (D,), jnp.float32, jnp.log(0.3), jnp.log(3.0)))
    pixel_scale = jnp.exp(jax.random.uniform(pixel_key, (REGIONS, REGION_ROWS, COLS, 1), jnp.float32, jnp.log(0.4), jnp.log(4.0)))
    base = jnp.clip(jax.random.normal(base_key, shape, jnp.float32), -4.0, 4.0)
    return (base * channel_scale * pixel_scale).astype(jnp.bfloat16)


def level_of(stream_key, extent, pieces, least, high):
    def one(axis_at, parts):
        steps = jax.random.uniform(jax.random.fold_in(jax.random.fold_in(stream_key, 6), axis_at), (parts,), jnp.float32, least / len(pieces), high / len(pieces))
        return jnp.repeat(jnp.exp(steps), extent[axis_at] // parts).reshape((-1,) + (1,) * (len(extent) - axis_at - 1))

    level = one(*pieces[0])
    for cut in pieces[1:]:
        level = level * one(*cut)
    return level


def noise(stream_key, shape, width, limit, cuts=(), held_as=jnp.bfloat16):
    drawn = width * jax.random.normal(stream_key, shape, jnp.float32)
    if cuts:
        drawn = drawn * level_of(stream_key, shape, cuts, -0.22, 0.18)
    return jnp.clip(drawn, -limit, limit).astype(held_as)


def setup_inputs(seed: int = 0) -> dict:
    key_list = jax.random.split(jax.random.key(seed), 9)
    return {
        "features": draw_features(jax.random.fold_in(key_list[8], 71), 0),
        "cotangent": noise(key_list[1], (REGIONS, REGION_ROWS, COLS, D), 1.0, 6.0, ((0, 8), (1, 4))),
        "dw_kernel": noise(key_list[2], (KW, KW, D), (KW * KW) ** -0.5, 0.875, (), jnp.float32),
        "ln_gain": jnp.clip(1.0 + 0.18 * jax.random.normal(key_list[3], (D,), jnp.float32), 0.1, 1.9),
        "ln_bias": noise(key_list[4], (D,), 0.5, 3.0, (), jnp.float32),
        "layer_scale": jnp.clip(jnp.exp(jax.random.uniform(key_list[5], (D,), jnp.float32, math.log(0.3), math.log(3.0))), 0.3, 3.0),
        "w_up": noise(key_list[6], (D, FF), D ** -0.5, 0.25, ((0, 8),)),
        "w_down": noise(key_list[7], (FF, D), FF ** -0.5, 0.125, ((0, 8),)),
    }


def gelu_pair(preact):
    cumulative = 0.5 * (1.0 + jax.scipy.special.erf(preact * (1.0 / math.sqrt(2.0))))
    density = jnp.exp(-0.5 * preact * preact) * (1.0 / math.sqrt(2.0 * math.pi))
    return (preact * cumulative, cumulative + preact * density)

def depthwise(padded, kernel, num_rows, num_cols):
    summed = jnp.zeros((num_rows, num_cols, padded.shape[-1]), jnp.float32)
    for row_off in range(kernel.shape[0]):
        for col_off in range(kernel.shape[1]):
            summed = summed + kernel[row_off, col_off] * padded[row_off:row_off + num_rows, col_off:col_off + num_cols]
    return summed

def kernel_grad(padded, upstream):
    num_rows, num_cols = (upstream.shape[0], upstream.shape[1])
    entries = []
    for row_off in range(KW):
        for col_off in range(KW):
            window = padded[row_off:row_off + num_rows, col_off:col_off + num_cols]
            entries.append(lax.optimization_barrier(jnp.sum(window * upstream, axis=(0, 1))))
    return jnp.stack(entries).reshape(KW, KW, upstream.shape[-1])

def normalize(conv_out, ln_gain, ln_bias):
    center = conv_out - lax.optimization_barrier(jnp.mean(conv_out, axis=-1, keepdims=True))
    inverse = lax.rsqrt(lax.optimization_barrier(jnp.mean(center * center, axis=-1, keepdims=True)) + 1e-06)
    scaled = center * inverse
    return (scaled, inverse, (scaled * ln_gain + ln_bias).astype(jnp.bfloat16))

def norm_back(d_norm, scaled, inverse, ln_gain):
    d_hat = d_norm * ln_gain
    first = lax.optimization_barrier(jnp.mean(d_hat, axis=-1, keepdims=True))
    second = lax.optimization_barrier(jnp.mean(d_hat * scaled, axis=-1, keepdims=True))
    return inverse * (d_hat - first - scaled * second)

def reference(features, cotangent, dw_kernel, ln_gain, ln_bias, layer_scale, w_up, w_down):
    margin = KW // 2
    flipped = dw_kernel[::-1, ::-1]

    def region_step(totals, inputs):
        region_x, region_cot = inputs
        num_rows, num_cols = (region_x.shape[0], region_x.shape[1])
        xfloat = region_x.astype(jnp.float32)
        padded = jnp.pad(xfloat, ((margin, margin), (margin, margin), (0, 0)))
        conv_out = depthwise(padded, dw_kernel, num_rows, num_cols)
        scaled, inverse, normed = normalize(conv_out, ln_gain, ln_bias)
        tokens = normed.reshape(-1, D)
        scaled_rows = scaled.reshape(-1, D)
        preact = jnp.dot(tokens, w_up, preferred_element_type=jnp.float32)
        activation, slope = gelu_pair(preact)
        hidden_act = activation.astype(jnp.bfloat16)
        mixed = jnp.dot(hidden_act, w_down, preferred_element_type=jnp.float32)
        result = (xfloat.reshape(-1, D) + layer_scale * mixed).astype(jnp.bfloat16)
        cot_rows = region_cot.reshape(-1, D).astype(jnp.float32)
        d_mixed = (layer_scale * cot_rows).astype(jnp.bfloat16)
        d_hidden = jnp.dot(d_mixed, w_down.T, preferred_element_type=jnp.float32)
        d_pre = (d_hidden * slope).astype(jnp.bfloat16)
        d_norm = jnp.dot(d_pre, w_up.T, preferred_element_type=jnp.float32)
        d_conv = norm_back(d_norm, scaled_rows, inverse.reshape(-1, 1), ln_gain).astype(jnp.bfloat16)
        d_conv = lax.optimization_barrier(d_conv)
        d_grid = d_conv.astype(jnp.float32).reshape(num_rows, num_cols, D)
        pad_grad = jnp.pad(d_grid, ((margin, margin), (margin, margin), (0, 0)))
        d_feat = cot_rows.reshape(num_rows, num_cols, D) + depthwise(pad_grad, flipped, num_rows, num_cols)
        grad_up, grad_down, grad_kernel, grad_gain, grad_bias, grad_scale = totals
        totals = (grad_up + jnp.dot(tokens.T, d_pre, preferred_element_type=jnp.float32), grad_down + jnp.dot(hidden_act.T, d_mixed, preferred_element_type=jnp.float32), grad_kernel + kernel_grad(padded, d_grid), grad_gain + lax.optimization_barrier(jnp.sum(d_norm * scaled_rows, axis=0)), grad_bias + lax.optimization_barrier(jnp.sum(d_norm, axis=0)), grad_scale + lax.optimization_barrier(jnp.sum(cot_rows * mixed, axis=0)))
        return (totals, (result.reshape(num_rows, num_cols, D), d_feat))
    zeros = (jnp.zeros((D, FF), jnp.float32), jnp.zeros((FF, D), jnp.float32), jnp.zeros((KW, KW, D), jnp.float32), jnp.zeros((D,), jnp.float32), jnp.zeros((D,), jnp.float32), jnp.zeros((D,), jnp.float32))
    totals, outputs = lax.scan(region_step, zeros, (features, cotangent))
    regions = float(N_DP)
    return (outputs[0], outputs[1], totals[0] / regions, totals[1] / regions, totals[2] / regions, totals[3] / regions, totals[4] / regions, totals[5] / regions)
```

```python
import functools
import math

import jax
import jax.numpy as jnp
from jax import lax
from jax.experimental import pallas as pl
from jax.experimental.pallas import tpu as pltpu
from jax.sharding import PartitionSpec as P

F32, BF16 = jnp.float32, jnp.bfloat16
LANES = 128
EDGE = 8


def gelu_pair(preact):
    cumulative = 0.5 * (1.0 + lax.erf(preact * (1.0 / math.sqrt(2.0))))
    density = jnp.exp(-0.5 * preact * preact) * (1.0 / math.sqrt(2.0 * math.pi))
    return (preact * cumulative, cumulative + preact * density)


def remote(src, dst, send_sem, recv_sem, device):
    return pltpu.make_async_remote_copy(
        src_ref=src,
        dst_ref=dst,
        send_sem=send_sem,
        recv_sem=recv_sem,
        device_id=device,
        device_id_type=pl.DeviceIdType.MESH,
    )


def block_kernel(
    sizes,
    x_ref, cot_ref, kern_ref, gain_ref, bias_ref, scale_ref, wup_ref, wdown_ref,
    res_ref, dfeat_ref, gup_ref, gdown_ref, small_ref,
    xpad, gpad, halo_x, halo_g, conv, scaled_ref, dconv, upg, tok, dmx, hid, dpre,
    part_n, part_m, r1n, r1m, chip_n, chip_m, r2n, r2m, own_n, own_m,
    gpart, gsend, grecv, fsend, frecv, small, ar1, ar2, ar3,
    hx_s, hx_r, hg_s, hg_r, w_s, w_r, dm_s, dm_r, tk_s, tk_r,
    an_s, an_r, am_s, am_r, bn_s, bn_r, bm_s, bm_r,
    gz_s, gz_r, fi_s, fi_r, s1_s, s1_r, s2_s, s2_r, s3_s, s3_r,
):
    n_dp, n_sp, rows, cols, width, taps = sizes
    chips, share = n_dp // 2, n_dp // n_sp
    margin = taps // 2
    pixels = rows * cols
    hidden = wdown_ref.shape[0]
    d, s = lax.axis_index("dp"), lax.axis_index("space")
    chip, core = d // 2, lax.rem(d, 2)
    sibling = chip * 2 + (1 - core)
    home = d // share
    place = lax.rem(d, share)
    inside = (home == s).astype(jnp.int32)

    def dp_peer(off):
        return lax.rem(d + off, n_dp)

    def sp_peer(off):
        return lax.rem(s + off, n_sp)

    barrier = pltpu.get_barrier_semaphore()

    def greet(device):
        pl.semaphore_signal(barrier, inc=1, device_id=device, device_id_type=pl.DeviceIdType.MESH)

    for off in range(1, n_dp):
        greet((dp_peer(off), s))
    for off in range(1, n_sp):
        greet((d, sp_peer(off)))
    for b in range(share):
        own_block = jnp.logical_and(home == s, place == b)

        @pl.when(jnp.logical_not(own_block))
        def _():
            greet((s * share + b, home))

    dmx[d] = (scale_ref[...] * cot_ref[...].astype(F32)).astype(BF16)
    pl.semaphore_wait(barrier, (n_dp - 1) + (n_sp - 1) + share - inside)

    has_up, has_down = s > 0, s < n_sp - 1

    def halo_copies(source, halo, send, recv):
        down = remote(source.at[pl.ds(rows - margin, margin)], halo.at[0], send.at[0], recv.at[0], (d, jnp.minimum(s + 1, n_sp - 1)))
        up = remote(source.at[pl.ds(0, margin)], halo.at[1], send.at[1], recv.at[1], (d, jnp.maximum(s - 1, 0)))
        return down, up

    def halo_start(copies):
        pl.when(has_down)(copies[0].start)
        pl.when(has_up)(copies[1].start)

    def halo_land(copies, halo, padded):
        @pl.when(has_up)
        def _():
            copies[0].wait_recv()
            padded[0:margin, EDGE:EDGE + cols] = halo[0].astype(F32)

        @pl.when(has_down)
        def _():
            copies[1].wait_recv()
            padded[rows + margin:, EDGE:EDGE + cols] = halo[1].astype(F32)

    def halo_sent(copies):
        pl.when(has_down)(copies[0].wait_send)
        pl.when(has_up)(copies[1].wait_send)

    hx = halo_copies(x_ref, halo_x, hx_s, hx_r)
    halo_start(hx)

    def spread(buf, send, recv):
        first = [remote(buf.at[d], buf.at[d], send.at[0], recv.at[d], (sibling, s))]
        for off in range(1, chips):
            first.append(remote(buf.at[d], buf.at[d], send.at[off], recv.at[d], (lax.rem(chip + off, chips) * 2 + core, s)))
        passed = []
        for off in range(1, chips):
            slot = lax.rem(chip + chips - off, chips) * 2 + core
            passed.append(remote(buf.at[slot], buf.at[slot], send.at[chips - 1 + off], recv.at[slot], (sibling, s)))
        last = []
        for off in range(chips):
            slot = lax.rem(chip + chips - off, chips) * 2 + (1 - core)
            last.append(remote(buf.at[slot], buf.at[slot], send.at[0], recv.at[slot], (sibling, s)))
        return first, passed, last

    dm_first, dm_passed, dm_last = spread(dmx, dm_s, dm_r)
    w_out = [remote(wup_ref.at[dp_peer(off)], upg.at[d], w_s.at[off], w_r.at[d], (dp_peer(off), s)) for off in range(1, n_dp)]
    w_in = [remote(wup_ref.at[dp_peer(off)], upg.at[dp_peer(off)], w_s.at[off], w_r.at[dp_peer(off)], (sibling, s)) for off in range(1, n_dp)]
    for copy in w_out:
        copy.start()
    for copy in dm_first:
        copy.start()
    upg[d] = wup_ref[d]

    wide = xpad.shape[1]
    for padded in (xpad, gpad):
        padded[...] = jnp.zeros(padded.shape, F32)
    xpad[margin:margin + rows, EDGE:EDGE + cols] = x_ref[...].astype(F32)
    halo_land(hx, halo_x, xpad)

    def convolve(padded, flip, lanes):
        total = jnp.zeros((rows, cols, LANES), F32)
        for b in range(taps):
            first = EDGE - margin + b
            window = padded[:, first:first + cols, lanes]
            for a in range(taps):
                tap = a * taps + b
                tap = taps * taps - 1 - tap if flip else tap
                total = total + kern_ref[tap:tap + 1, lanes].reshape(1, 1, LANES) * window[a:a + rows]
        return total

    def lanes_of(c):
        return pl.ds(pl.multiple_of(c * LANES, LANES), LANES)

    @pl.loop(0, width // LANES)
    def _(c):
        conv[:, lanes_of(c)] = convolve(xpad, False, lanes_of(c)).reshape(pixels, LANES)

    center = conv[...]
    center = center - jnp.mean(center, axis=-1, keepdims=True)
    inverse = lax.rsqrt(jnp.mean(center * center, axis=-1, keepdims=True) + 1e-06)
    normal = center * inverse
    scaled_ref[...] = normal
    tok[d] = (normal * gain_ref[...] + bias_ref[...]).astype(BF16)

    tk_first, tk_passed, tk_last = spread(tok, tk_s, tk_r)
    for copy in tk_first:
        copy.start()
    for group in (dm_passed, tk_passed):
        for copy in group:
            copy.wait_recv()
            copy.start()
    for copy in w_in:
        copy.wait_recv()
    for group in (dm_last, tk_last):
        for copy in group:
            copy.wait_recv()

    def nn(a, b):
        return lax.dot_general(a, b, (((1,), (0,)), ((), ())), preferred_element_type=F32)

    def nt(a, b):
        return lax.dot_general(a, b, (((1,), (1,)), ((), ())), preferred_element_type=F32)

    def tn(a, b):
        return lax.dot_general(a, b, (((0,), (0,)), ((), ())), preferred_element_type=F32)

    def cross(kind, to):
        buf, got, send, recv = kind
        return remote(buf.at[to], got.at[to], send.at[to], recv.at[to], (sibling, s))

    def home_copy(kind, to):
        buf, got, send, recv = kind
        return remote(buf.at[to], got.at[chip], send.at[to], recv.at[chip], (to * 2 + core, s))

    cross_n, cross_m = (part_n, r1n, an_s, an_r), (part_m, r1m, am_s, am_r)
    home_n, home_m = (chip_n, r2n, bn_s, bn_r), (chip_m, r2m, bm_s, bm_r)

    def products(slot):
        up = upg[...].reshape(width, hidden)
        activation, slope = gelu_pair(nn(tok[slot], up))
        act = activation.astype(BF16)
        grad = (nt(dmx[slot], wdown_ref[...]) * slope).astype(BF16)
        hid[slot] = act
        dpre[slot] = grad
        return nt(grad, up), nn(act, wdown_ref[...])

    @pl.loop(0, chips)
    def _(i):
        to = lax.rem(chip + 1 + i, chips)
        normed, mixed = products(to * 2 + (1 - core))
        part_n[to] = normed.astype(BF16)
        cross(cross_n, to).start()
        part_m[to] = mixed.astype(BF16)
        cross(cross_m, to).start()

    @pl.loop(0, chips - 1)
    def _(i):
        to = lax.rem(chip + 1 + i, chips)
        normed, mixed = products(to * 2 + core)
        cross(cross_n, to).wait_recv()
        chip_n[to] = (normed + r1n[to].astype(F32)).astype(BF16)
        home_copy(home_n, to).start()
        cross(cross_m, to).wait_recv()
        chip_m[to] = (mixed + r1m[to].astype(F32)).astype(BF16)
        home_copy(home_m, to).start()

    normed, mixed = products(d)
    cross(cross_n, chip).wait_recv()
    own_n[...] = normed + r1n[chip].astype(F32)
    cross(cross_m, chip).wait_recv()
    own_m[...] = mixed + r1m[chip].astype(F32)

    strip = width // n_sp
    part_rows = strip // share
    flat = (n_dp * pixels,)
    for which, (left, right) in enumerate(((tok, dpre), (dmx, hid))):
        gpart[which] = tn(left[...].reshape(flat + (width,)), right[...].reshape(flat + (hidden,)))
        for k in range(n_sp):
            gsend[k, which] = gpart[which, k * strip:(k + 1) * strip].astype(BF16)
    gz_out = [remote(gsend.at[sp_peer(off)], grecv.at[s], gz_s.at[off], gz_r.at[s], (d, sp_peer(off))) for off in range(1, n_sp)]
    gz_in = [remote(gsend.at[sp_peer(off)], grecv.at[sp_peer(off)], gz_s.at[off], gz_r.at[sp_peer(off)], (d, sp_peer(off))) for off in range(1, n_sp)]
    for copy in gz_out:
        copy.start()

    def arrive(got, send, recv, own):
        total = own[...]
        for off in range(1, chips):
            source = lax.rem(chip + off, chips)
            remote(got.at[source], got.at[source], send.at[source], recv.at[source], (sibling, s)).wait_recv()
            total = total + got[source].astype(F32)
        return total

    d_norm = arrive(r2n, bn_s, bn_r, own_n)
    normal = scaled_ref[...]
    d_hat = d_norm * gain_ref[...]
    lead = jnp.mean(d_hat, axis=-1, keepdims=True)
    second = jnp.mean(d_hat * normal, axis=-1, keepdims=True)
    dconv[...] = (inverse * (d_hat - lead - normal * second)).astype(BF16).reshape(rows, cols, width)
    hg = halo_copies(dconv, halo_g, hg_s, hg_r)
    halo_start(hg)
    gpad[margin:margin + rows, EDGE:EDGE + cols] = dconv[...].astype(F32)

    per = small.shape[1]
    count = taps * taps

    def put(row, lanes, value):
        small[row // per, row % per:row % per + 1, lanes] = value

    small[...] = jnp.zeros(small.shape, F32)
    everything = slice(None)
    put(count, everything, jnp.sum(d_norm * normal, axis=0, keepdims=True))
    put(count + 1, everything, jnp.sum(d_norm, axis=0, keepdims=True))

    @pl.loop(0, width // LANES)
    def _(c):
        lanes = lanes_of(c)
        upstream = gpad[margin:margin + rows, EDGE:EDGE + cols, lanes]
        for b in range(taps):
            first = EDGE - margin + b
            window = xpad[:, first:first + cols, lanes]
            for a in range(taps):
                product = jnp.sum(window[a:a + rows] * upstream, axis=0)
                put(a * taps + b, lanes, jnp.sum(product, axis=0, keepdims=True))

    mixed = arrive(r2m, bm_s, bm_r, own_m)
    res_ref[...] = (x_ref[...].reshape(pixels, width).astype(F32) + scale_ref[...] * mixed).astype(BF16).reshape(rows, cols, width)
    put(count + 2, everything, jnp.sum(cot_ref[...].astype(F32) * mixed, axis=0, keepdims=True))

    s1_out = [remote(small.at[dp_peer(off)], ar1.at[d], s1_s.at[off], s1_r.at[d], (dp_peer(off), s)) for off in range(1, n_dp)]
    s1_in = [remote(small.at[dp_peer(off)], ar1.at[dp_peer(off)], s1_s.at[off], s1_r.at[dp_peer(off)], (sibling, s)) for off in range(1, n_dp)]
    for copy in s1_out:
        copy.start()
    ar1[d] = small[d]

    for copy in gz_in:
        copy.wait_recv()
    for which in range(2):
        total = gpart[which, pl.ds(pl.multiple_of(s * strip, strip), strip)]
        for off in range(1, n_sp):
            total = total + grecv[sp_peer(off), which].astype(F32)
        for b in range(share):
            fsend[b, which] = total[b * part_rows:(b + 1) * part_rows].astype(BF16)
    for b in range(share):
        own_block = jnp.logical_and(home == s, place == b)
        copy = remote(fsend.at[b], frecv.at[place], fi_s.at[b], fi_r.at[place], (s * share + b, home))

        pl.when(jnp.logical_not(own_block))(copy.start)

        @pl.when(own_block)
        def _():
            frecv[b] = fsend[b]

    for copy in s1_in:
        copy.wait_recv()
    ar2[s] = jnp.sum(ar1[...], axis=0)
    s2_out = [remote(ar2.at[s], ar2.at[s], s2_s.at[off], s2_r.at[s], (d, sp_peer(off))) for off in range(1, n_sp)]
    s2_in = [remote(ar2.at[s], ar2.at[sp_peer(off)], s2_s.at[off], s2_r.at[sp_peer(off)], (d, sp_peer(off))) for off in range(1, n_sp)]
    for copy in s2_out:
        copy.start()

    halo_land(hg, halo_g, gpad)

    @pl.loop(0, width // LANES)
    def _(c):
        lanes = lanes_of(c)
        cot = cot_ref[:, lanes].astype(F32).reshape(rows, cols, LANES)
        dfeat_ref[:, :, lanes] = cot + convolve(gpad, True, lanes)

    for copy in s2_in:
        copy.wait_recv()
    ar3[d] = jnp.sum(ar2[...], axis=0)
    s3_out = [remote(ar3.at[d], ar3.at[d], s3_s.at[off], s3_r.at[d], (dp_peer(off), s)) for off in range(1, n_dp)]
    s3_in = [remote(ar3.at[d], ar3.at[dp_peer(off)], s3_s.at[off], s3_r.at[dp_peer(off)], (sibling, s)) for off in range(1, n_dp)]
    for copy in s3_out:
        copy.start()

    for b in range(share):
        own_block = jnp.logical_and(home == s, place == b)
        copy = remote(fsend.at[b], frecv.at[b], fi_s.at[b], fi_r.at[b], (s * share + b, home))
        pl.when(jnp.logical_not(own_block))(copy.wait_recv)
    for b in range(share):
        gup_ref[:, b * hidden:(b + 1) * hidden] = frecv[b, 0].astype(F32)
        gdown_ref[:, b * hidden:(b + 1) * hidden] = frecv[b, 1].astype(F32)

    for copy in s3_in:
        copy.wait_recv()
    small_ref[...] = ar3[...]

    halo_sent(hx)
    halo_sent(hg)
    for group in (w_out, dm_first, dm_passed, tk_first, tk_passed, gz_out, s1_out, s2_out, s3_out):
        for copy in group:
            copy.wait_send()
    for b in range(share):
        own_block = jnp.logical_and(home == s, place == b)
        copy = remote(fsend.at[b], frecv.at[b], fi_s.at[b], fi_r.at[b], (s * share + b, home))
        pl.when(jnp.logical_not(own_block))(copy.wait_send)

    for off in range(chips):
        to = lax.rem(chip + 1 + off, chips)
        cross(cross_n, to).wait_send()
        cross(cross_m, to).wait_send()
        if off < chips - 1:
            home_copy(home_n, to).wait_send()
            home_copy(home_m, to).wait_send()


def local(features, cotangent, dw_kernel, ln_gain, ln_bias, layer_scale, w_up, w_down):
    n_dp, n_sp = lax.axis_size("dp"), lax.axis_size("space")
    _, rows, cols, width = features.shape
    taps = dw_kernel.shape[0]
    margin = taps // 2
    pixels = rows * cols
    hidden = w_down.shape[0]
    chips, share = n_dp // 2, n_dp // n_sp
    strip = width // n_sp
    part_rows = strip // share
    count = taps * taps
    per = -(-(count + 3) // n_dp)
    outgoing = w_up.reshape(w_up.shape[0], n_dp, hidden).transpose(1, 0, 2)
    padded = (rows + 2 * margin, cols + 2 * EDGE, width)
    dma = lambda k: pltpu.SemaphoreType.DMA((k,))
    vm = pltpu.VMEM
    scratch = [
        vm(padded, F32), vm(padded, F32),
        vm((2, margin, cols, width), BF16), vm((2, margin, cols, width), BF16),
        vm((pixels, width), F32), vm((pixels, width), F32), vm((rows, cols, width), BF16),
        vm(outgoing.shape, BF16),
        vm((n_dp, pixels, width), BF16), vm((n_dp, pixels, width), BF16),
        vm((n_dp, pixels, hidden), BF16), vm((n_dp, pixels, hidden), BF16),
    ]
    scratch += [vm((chips, pixels, width), BF16)] * 8
    scratch += [vm((pixels, width), F32)] * 2
    scratch += [
        vm((2, width, hidden), F32),
        vm((n_sp, 2, strip, hidden), BF16), vm((n_sp, 2, strip, hidden), BF16),
        vm((share, 2, part_rows, hidden), BF16), vm((share, 2, part_rows, hidden), BF16),
        vm((n_dp, per, width), F32), vm((n_dp, per, width), F32),
        vm((n_sp, per, width), F32), vm((n_dp, per, width), F32),
    ]
    scratch += [dma(2)] * 4 + [dma(n_dp)] * 6 + [dma(chips)] * 8
    scratch += [dma(n_sp)] * 2 + [dma(share)] * 2 + [dma(n_dp)] * 2 + [dma(n_sp)] * 2 + [dma(n_dp)] * 2
    whole = pl.BlockSpec(memory_space=pltpu.VMEM)
    result, d_feat, grad_up, grad_down, small = pl.pallas_call(
        functools.partial(block_kernel, (n_dp, n_sp, rows, cols, width, taps)),
        out_shape=(
            jax.ShapeDtypeStruct((rows, cols, width), BF16),
            jax.ShapeDtypeStruct((rows, cols, width), F32),
            jax.ShapeDtypeStruct((part_rows, share * hidden), F32),
            jax.ShapeDtypeStruct((part_rows, share * hidden), F32),
            jax.ShapeDtypeStruct((n_dp, per, width), F32),
        ),
        in_specs=[whole] * 8,
        out_specs=(whole,) * 5,
        scratch_shapes=scratch,
        compiler_params=pltpu.CompilerParams(
            collective_id=0, has_side_effects=True, vmem_limit_bytes=60 << 20
        ),
    )(
        features[0],
        cotangent[0].reshape(pixels, width),
        dw_kernel.reshape(count, width),
        ln_gain.reshape(1, width),
        ln_bias.reshape(1, width),
        layer_scale.reshape(1, width),
        outgoing,
        w_down,
    )
    regions = float(n_dp)
    small = small.reshape(n_dp * per, width) / regions
    return (
        result[None],
        d_feat[None],
        grad_up / regions,
        grad_down.T / regions,
        small[:count].reshape(taps, taps, width),
        small[count],
        small[count + 1],
        small[count + 2],
    )


def solution(mesh):
    in_specs = (
        P("dp", "space", None, None),
        P("dp", "space", None, None),
        P(),
        P(),
        P(),
        P(),
        P("dp", None),
        P("dp", None),
    )
    out_specs = (
        P("dp", "space", None, None),
        P("dp", "space", None, None),
        P("dp", "space"),
        P("space", "dp"),
        P(),
        P(),
        P(),
        P(),
    )
    return jax.shard_map(local, mesh=mesh, in_specs=in_specs, out_specs=out_specs, check_vma=False)
```

```python
import functools
import math

import jax
import jax.numpy as jnp
from jax import lax
from jax.experimental import pallas as pl
from jax.experimental.pallas import tpu as pltpu
from jax.sharding import PartitionSpec as P

F32, BF16 = jnp.float32, jnp.bfloat16
LANES = 128
EDGE = 8


def gelu_pair(preact):
    cumulative = 0.5 * (1.0 + lax.erf(preact * (1.0 / math.sqrt(2.0))))
    density = jnp.exp(-0.5 * preact * preact) * (1.0 / math.sqrt(2.0 * math.pi))
    return (preact * cumulative, cumulative + preact * density)


def remote(src, dst, send_sem, recv_sem, device):
    return pltpu.make_async_remote_copy(
        src_ref=src,
        dst_ref=dst,
        send_sem=send_sem,
        recv_sem=recv_sem,
        device_id=device,
        device_id_type=pl.DeviceIdType.MESH,
    )


def block_kernel(
    sizes,
    x_ref, cot_ref, kern_ref, gain_ref, bias_ref, scale_ref, wup_ref, wdown_ref,
    res_ref, dfeat_ref, gup_ref, gdown_ref, gkern_ref, ggain_ref, gbias_ref, gscale_ref,
    xpad, gpad, halo_x, halo_g, conv, scaled_ref, dconv, wout, upg, tok, dmx, hid, dpre,
    part_n, part_m, r1n, r1m, chip_n, chip_m, r2n, r2m, own_n, own_m,
    gsend, grecv, dscale, small, ar1, ar2, ar3,
    hx_s, hx_r, hg_s, hg_r, w_s, w_r, dm_s, dm_r, tk_s, tk_r,
    an_s, an_r, am_s, am_r, bn_s, bn_r, bm_s, bm_r,
    gz_s, gz_r, s1_s, s1_r, s2_s, s2_r, s3_s, s3_r,
):
    n_dp, n_sp, rows, cols, width, taps = sizes
    chips, share = n_dp // 2, n_dp // n_sp
    margin = taps // 2
    pixels = rows * cols
    hidden = wdown_ref.shape[0]
    d, s = lax.axis_index("dp"), lax.axis_index("space")
    chip, core = d // 2, lax.rem(d, 2)
    sibling = chip * 2 + (1 - core)
    home = d // share
    place = lax.rem(d, share)
    inside = (home == s).astype(jnp.int32)

    def is_self(j, k):
        return jnp.logical_and(jnp.logical_and(home == s, place == j), s == k)

    def dp_peer(off):
        return lax.rem(d + off, n_dp)

    def sp_peer(off):
        return lax.rem(s + off, n_sp)

    barrier = pltpu.get_barrier_semaphore()

    def greet(device):
        pl.semaphore_signal(barrier, inc=1, device_id=device, device_id_type=pl.DeviceIdType.MESH)

    for off in range(1, n_dp):
        greet((dp_peer(off), s))
    for off in range(1, n_sp):
        greet((d, sp_peer(off)))
    for j in range(share):
        for k in range(n_sp):
            @pl.when(jnp.logical_not(is_self(j, k)))
            def _():
                greet((s * share + j, jnp.int32(k)))

    dmx[d] = (scale_ref[...] * cot_ref[...].astype(F32)).astype(BF16)
    for t in range(n_dp):
        wout[t] = wup_ref[:, t * hidden:(t + 1) * hidden]
    upg[d] = wout[d]
    for padded in (xpad, gpad):
        padded[...] = jnp.zeros(padded.shape, F32)
    xpad[margin:margin + rows, EDGE:EDGE + cols] = x_ref[...].astype(F32)
    dscale[...] = jnp.zeros(dscale.shape, F32)
    small[...] = jnp.zeros(small.shape, F32)
    pl.semaphore_wait(barrier, (n_dp - 1) + (n_sp - 1) + n_dp - inside)

    has_up, has_down = s > 0, s < n_sp - 1

    def halo_copies(source, halo, send, recv):
        down = remote(source.at[pl.ds(rows - margin, margin)], halo.at[0], send.at[0], recv.at[0], (d, jnp.minimum(s + 1, n_sp - 1)))
        up = remote(source.at[pl.ds(0, margin)], halo.at[1], send.at[1], recv.at[1], (d, jnp.maximum(s - 1, 0)))
        return down, up

    def halo_start(copies):
        pl.when(has_down)(copies[0].start)
        pl.when(has_up)(copies[1].start)

    def halo_land(copies, halo, padded):
        @pl.when(has_up)
        def _():
            copies[0].wait_recv()
            padded[0:margin, EDGE:EDGE + cols] = halo[0].astype(F32)

        @pl.when(has_down)
        def _():
            copies[1].wait_recv()
            padded[rows + margin:, EDGE:EDGE + cols] = halo[1].astype(F32)

    def halo_sent(copies):
        pl.when(has_down)(copies[0].wait_send)
        pl.when(has_up)(copies[1].wait_send)

    hx = halo_copies(x_ref, halo_x, hx_s, hx_r)
    halo_start(hx)

    def spread(buf, send, recv):
        first = [remote(buf.at[d], buf.at[d], send.at[0], recv.at[d], (sibling, s))]
        for off in range(1, chips):
            first.append(remote(buf.at[d], buf.at[d], send.at[off], recv.at[d], (lax.rem(chip + off, chips) * 2 + core, s)))
        passed = []
        for off in range(1, chips):
            slot = lax.rem(chip + chips - off, chips) * 2 + core
            passed.append(remote(buf.at[slot], buf.at[slot], send.at[chips - 1 + off], recv.at[slot], (sibling, s)))
        last = []
        for off in range(chips):
            slot = lax.rem(chip + chips - off, chips) * 2 + (1 - core)
            last.append(remote(buf.at[slot], buf.at[slot], send.at[0], recv.at[slot], (sibling, s)))
        return first, passed, last

    dm_first, dm_passed, dm_last = spread(dmx, dm_s, dm_r)
    w_out = [remote(wout.at[dp_peer(off)], upg.at[d], w_s.at[off], w_r.at[d], (dp_peer(off), s)) for off in range(1, n_dp)]
    w_in = [remote(wout.at[dp_peer(off)], upg.at[dp_peer(off)], w_s.at[off], w_r.at[dp_peer(off)], (sibling, s)) for off in range(1, n_dp)]
    for copy in w_out:
        copy.start()
    for copy in dm_first:
        copy.start()

    halo_land(hx, halo_x, xpad)

    def convolve(padded, flip, lanes):
        total = jnp.zeros((rows, cols, LANES), F32)
        for b in range(taps):
            first = EDGE - margin + b
            window = padded[:, first:first + cols, lanes]
            for a in range(taps):
                at = (taps - 1 - a, taps - 1 - b) if flip else (a, b)
                tap = kern_ref[at[0], at[1]:at[1] + 1, lanes].reshape(1, 1, LANES)
                total = total + tap * window[a:a + rows]
        return total

    def lanes_of(c):
        return pl.ds(pl.multiple_of(c * LANES, LANES), LANES)

    @pl.loop(0, width // LANES)
    def _(c):
        conv[:, lanes_of(c)] = convolve(xpad, False, lanes_of(c)).reshape(pixels, LANES)

    center = conv[...]
    center = center - jnp.mean(center, axis=-1, keepdims=True)
    inverse = lax.rsqrt(jnp.mean(center * center, axis=-1, keepdims=True) + 1e-06)
    normal = center * inverse
    scaled_ref[...] = normal
    tok[d] = (normal * gain_ref[...] + bias_ref[...]).astype(BF16)

    tk_first, tk_passed, tk_last = spread(tok, tk_s, tk_r)
    for copy in tk_first:
        copy.start()
    for group in (dm_passed, tk_passed):
        for copy in group:
            copy.wait_recv()
            copy.start()
    for copy in w_in:
        copy.wait_recv()
    for group in (dm_last, tk_last):
        for copy in group:
            copy.wait_recv()

    def nn(a, b):
        return lax.dot_general(a, b, (((1,), (0,)), ((), ())), preferred_element_type=F32)

    def nt(a, b):
        return lax.dot_general(a, b, (((1,), (1,)), ((), ())), preferred_element_type=F32)

    def tn(a, b):
        return lax.dot_general(a, b, (((0,), (0,)), ((), ())), preferred_element_type=F32)

    def cross(kind, to):
        buf, got, send, recv = kind
        return remote(buf.at[to], got.at[to], send.at[to], recv.at[to], (sibling, s))

    def home_copy(kind, to):
        buf, got, send, recv = kind
        return remote(buf.at[to], got.at[chip], send.at[to], recv.at[chip], (to * 2 + core, s))

    cross_n, cross_m = (part_n, r1n, an_s, an_r), (part_m, r1m, am_s, am_r)
    home_n, home_m = (chip_n, r2n, bn_s, bn_r), (chip_m, r2m, bm_s, bm_r)

    def products(slot):
        up = upg[...].reshape(width, hidden)
        activation, slope = gelu_pair(nn(tok[slot], up))
        act = activation.astype(BF16)
        grad = (nt(dmx[slot], wdown_ref[...]) * slope).astype(BF16)
        hid[slot] = act
        dpre[slot] = grad
        mixed = nn(act, wdown_ref[...])
        dscale[...] += jnp.sum(dmx[slot].astype(F32) * mixed, axis=0, keepdims=True)
        return nt(grad, up), mixed

    @pl.loop(0, chips)
    def _(i):
        to = lax.rem(chip + 1 + i, chips)
        normed, mixed = products(to * 2 + (1 - core))
        part_n[to] = normed.astype(BF16)
        cross(cross_n, to).start()
        part_m[to] = mixed.astype(BF16)
        cross(cross_m, to).start()

    @pl.loop(0, chips - 1)
    def _(i):
        to = lax.rem(chip + 1 + i, chips)
        normed, mixed = products(to * 2 + core)
        cross(cross_n, to).wait_recv()
        chip_n[to] = (normed + r1n[to].astype(F32)).astype(BF16)
        home_copy(home_n, to).start()
        cross(cross_m, to).wait_recv()
        chip_m[to] = (mixed + r1m[to].astype(F32)).astype(BF16)

    normed, mixed = products(d)
    cross(cross_n, chip).wait_recv()
    own_n[...] = normed + r1n[chip].astype(F32)
    cross(cross_m, chip).wait_recv()
    own_m[...] = mixed + r1m[chip].astype(F32)

    part_rows = gsend.shape[2]
    flat = (n_dp * pixels,)
    for which, (left, right) in enumerate(((tok, dpre), (dmx, hid))):
        summed = tn(left[...].reshape(flat + (width,)), right[...].reshape(flat + (hidden,)))
        for t in range(n_dp):
            gsend[t, which] = summed[t * part_rows:(t + 1) * part_rows].astype(BF16)
    slot_out = place * n_sp + s
    own_home = home == s

    def owner_copy(off):
        to = dp_peer(off)
        return remote(gsend.at[to], grecv.at[slot_out], gz_s.at[off], gz_r.at[slot_out], (to, home))

    for off in range(1, n_dp):
        owner_copy(off).start()
    pl.when(jnp.logical_not(own_home))(owner_copy(0).start)

    @pl.when(own_home)
    def _():
        grecv[slot_out] = gsend[d]

    def arrive(got, send, recv, own):
        total = own[...]
        for off in range(1, chips):
            source = lax.rem(chip + off, chips)
            remote(got.at[source], got.at[source], send.at[source], recv.at[source], (sibling, s)).wait_recv()
            total = total + got[source].astype(F32)
        return total

    d_norm = arrive(r2n, bn_s, bn_r, own_n)
    for off in range(1, chips):
        home_copy(home_m, lax.rem(chip + off, chips)).start()
    normal = scaled_ref[...]
    d_hat = d_norm * gain_ref[...]
    lead = jnp.mean(d_hat, axis=-1, keepdims=True)
    second = jnp.mean(d_hat * normal, axis=-1, keepdims=True)
    dconv[...] = (inverse * (d_hat - lead - normal * second)).astype(BF16).reshape(rows, cols, width)
    hg = halo_copies(dconv, halo_g, hg_s, hg_r)
    halo_start(hg)
    gpad[margin:margin + rows, EDGE:EDGE + cols] = dconv[...].astype(F32)

    per = small.shape[1]
    count = taps * taps

    def put(row, lanes, value):
        small[row // per, row % per:row % per + 1, lanes] = value

    everything = slice(None)
    put(count, everything, jnp.sum(d_norm * normal, axis=0, keepdims=True))
    put(count + 1, everything, jnp.sum(d_norm, axis=0, keepdims=True))
    put(count + 2, everything, dscale[...] / scale_ref[...])

    @pl.loop(0, width // LANES)
    def _(c):
        lanes = lanes_of(c)
        upstream = gpad[margin:margin + rows, EDGE:EDGE + cols, lanes]
        for b in range(taps):
            first = EDGE - margin + b
            window = xpad[:, first:first + cols, lanes]
            for a in range(taps):
                product = jnp.sum(window[a:a + rows] * upstream, axis=0)
                put(a * taps + b, lanes, jnp.sum(product, axis=0, keepdims=True))

    s1_out = [remote(small.at[dp_peer(off)], ar1.at[d], s1_s.at[off], s1_r.at[d], (dp_peer(off), s)) for off in range(1, n_dp)]
    s1_in = [remote(small.at[dp_peer(off)], ar1.at[dp_peer(off)], s1_s.at[off], s1_r.at[dp_peer(off)], (sibling, s)) for off in range(1, n_dp)]
    for copy in s1_out:
        copy.start()
    ar1[d] = small[d]

    halo_land(hg, halo_g, gpad)

    @pl.loop(0, width // LANES)
    def _(c):
        lanes = lanes_of(c)
        cot = cot_ref[:, lanes].astype(F32).reshape(rows, cols, LANES)
        dfeat_ref[:, :, lanes] = cot + convolve(gpad, True, lanes)

    for copy in s1_in:
        copy.wait_recv()
    ar2[s] = jnp.sum(ar1[...], axis=0)
    s2_out = [remote(ar2.at[s], ar2.at[s], s2_s.at[off], s2_r.at[s], (d, sp_peer(off))) for off in range(1, n_sp)]
    s2_in = [remote(ar2.at[s], ar2.at[sp_peer(off)], s2_s.at[off], s2_r.at[sp_peer(off)], (d, sp_peer(off))) for off in range(1, n_sp)]
    for copy in s2_out:
        copy.start()

    mixed = arrive(r2m, bm_s, bm_r, own_m)
    res_ref[...] = (x_ref[...].reshape(pixels, width).astype(F32) + scale_ref[...] * mixed).astype(BF16).reshape(rows, cols, width)

    for copy in s2_in:
        copy.wait_recv()
    ar3[d] = jnp.sum(ar2[...], axis=0)
    s3_out = [remote(ar3.at[d], ar3.at[d], s3_s.at[off], s3_r.at[d], (dp_peer(off), s)) for off in range(1, n_dp)]
    s3_in = [remote(ar3.at[d], ar3.at[dp_peer(off)], s3_s.at[off], s3_r.at[dp_peer(off)], (sibling, s)) for off in range(1, n_dp)]
    for copy in s3_out:
        copy.start()

    for j in range(share):
        sums = [None, None]
        for k in range(n_sp):
            slot = j * n_sp + k
            landed = remote(gsend.at[0], grecv.at[slot], gz_s.at[0], gz_r.at[slot], (sibling, s))
            pl.when(jnp.logical_not(is_self(j, k)))(landed.wait_recv)
            for which in range(2):
                part = grecv[slot, which].astype(F32)
                sums[which] = part if k == 0 else sums[which] + part
        gup_ref[:, j * hidden:(j + 1) * hidden] = sums[0]
        gdown_ref[:, j * hidden:(j + 1) * hidden] = sums[1]

    for copy in s3_in:
        copy.wait_recv()

    def take(row):
        return ar3[row // per, row % per:row % per + 1]

    for a in range(taps):
        for b in range(taps):
            gkern_ref[a, b:b + 1] = take(a * taps + b)
    ggain_ref[...] = take(count)
    gbias_ref[...] = take(count + 1)
    gscale_ref[...] = take(count + 2)

    halo_sent(hx)
    halo_sent(hg)
    for group in (w_out, dm_first, dm_passed, tk_first, tk_passed, s1_out, s2_out, s3_out):
        for copy in group:
            copy.wait_send()
    for off in range(1, n_dp):
        owner_copy(off).wait_send()
    pl.when(jnp.logical_not(own_home))(owner_copy(0).wait_send)

    for off in range(chips):
        to = lax.rem(chip + 1 + off, chips)
        cross(cross_n, to).wait_send()
        cross(cross_m, to).wait_send()
        if off < chips - 1:
            home_copy(home_n, to).wait_send()
            home_copy(home_m, to).wait_send()


def local(features, cotangent, dw_kernel, ln_gain, ln_bias, layer_scale, w_up, w_down):
    n_dp, n_sp = lax.axis_size("dp"), lax.axis_size("space")
    _, rows, cols, width = features.shape
    taps = dw_kernel.shape[0]
    margin = taps // 2
    pixels = rows * cols
    hidden = w_down.shape[0]
    chips, share = n_dp // 2, n_dp // n_sp
    part_rows = width // n_dp
    count = taps * taps
    per = -(-(count + 3) // n_dp)
    blocks = (n_dp, w_up.shape[0], hidden)
    padded = (rows + 2 * margin, cols + 2 * EDGE, width)
    dma = lambda k: pltpu.SemaphoreType.DMA((k,))
    vm = pltpu.VMEM
    scratch = [
        vm(padded, F32), vm(padded, F32),
        vm((2, margin, cols, width), BF16), vm((2, margin, cols, width), BF16),
        vm((pixels, width), F32), vm((pixels, width), F32), vm((rows, cols, width), BF16),
        vm(blocks, BF16), vm(blocks, BF16),
        vm((n_dp, pixels, width), BF16), vm((n_dp, pixels, width), BF16),
        vm((n_dp, pixels, hidden), BF16), vm((n_dp, pixels, hidden), BF16),
    ]
    scratch += [vm((chips, pixels, width), BF16)] * 8
    scratch += [vm((pixels, width), F32)] * 2
    scratch += [
        vm((n_dp, 2, part_rows, hidden), BF16), vm((n_dp, 2, part_rows, hidden), BF16),
        vm((1, width), F32),
        vm((n_dp, per, width), F32), vm((n_dp, per, width), F32),
        vm((n_sp, per, width), F32), vm((n_dp, per, width), F32),
    ]
    scratch += [dma(2)] * 4 + [dma(n_dp)] * 6 + [dma(chips)] * 8
    scratch += [dma(n_dp)] * 4 + [dma(n_sp)] * 2 + [dma(n_dp)] * 2
    whole = pl.BlockSpec(memory_space=pltpu.VMEM)
    result, d_feat, grad_up, grad_down, kernel_sum, gain_sum, bias_sum, scale_sum = pl.pallas_call(
        functools.partial(block_kernel, (n_dp, n_sp, rows, cols, width, taps)),
        out_shape=(
            jax.ShapeDtypeStruct((rows, cols, width), BF16),
            jax.ShapeDtypeStruct((rows, cols, width), F32),
            jax.ShapeDtypeStruct((part_rows, share * hidden), F32),
            jax.ShapeDtypeStruct((part_rows, share * hidden), F32),
            jax.ShapeDtypeStruct((taps, taps, width), F32),
        )
        + (jax.ShapeDtypeStruct((1, width), F32),) * 3,
        in_specs=[whole] * 8,
        out_specs=(whole,) * 8,
        scratch_shapes=scratch,
        compiler_params=pltpu.CompilerParams(
            collective_id=0, has_side_effects=True, vmem_limit_bytes=60 << 20
        ),
    )(
        features[0],
        cotangent[0].reshape(pixels, width),
        dw_kernel,
        ln_gain.reshape(1, width),
        ln_bias.reshape(1, width),
        layer_scale.reshape(1, width),
        w_up,
        w_down,
    )
    regions = float(n_dp)
    return (
        result[None],
        d_feat[None],
        grad_up / regions,
        grad_down.T / regions,
        kernel_sum / regions,
        gain_sum[0] / regions,
        bias_sum[0] / regions,
        scale_sum[0] / regions,
    )


def solution(mesh):
    in_specs = (
        P("dp", "space", None, None),
        P("dp", "space", None, None),
        P(),
        P(),
        P(),
        P(),
        P("dp", None),
        P("dp", None),
    )
    out_specs = (
        P("dp", "space", None, None),
        P("dp", "space", None, None),
        P("dp", "space"),
        P("space", "dp"),
        P(),
        P(),
        P(),
        P(),
    )
    return jax.shard_map(local, mesh=mesh, in_specs=in_specs, out_specs=out_specs, check_vma=False)
```

```python
import functools
import math

import jax
import jax.numpy as jnp
from jax import lax
from jax.experimental import pallas as pl
from jax.experimental.pallas import tpu as pltpu
from jax.sharding import PartitionSpec as P

F32, BF16 = jnp.float32, jnp.bfloat16
LANES = 128
EDGE = 8


def gelu_pair(preact):
    cumulative = 0.5 * (1.0 + lax.erf(preact * (1.0 / math.sqrt(2.0))))
    density = jnp.exp(-0.5 * preact * preact) * (1.0 / math.sqrt(2.0 * math.pi))
    return (preact * cumulative, cumulative + preact * density)


def remote(src, dst, send_sem, recv_sem, device):
    return pltpu.make_async_remote_copy(
        src_ref=src,
        dst_ref=dst,
        send_sem=send_sem,
        recv_sem=recv_sem,
        device_id=device,
        device_id_type=pl.DeviceIdType.MESH,
    )


def block_kernel(
    sizes,
    x_ref, cot_ref, kern_ref, gain_ref, bias_ref, scale_ref, wup_ref, wdown_ref,
    res_ref, dfeat_ref, gup_ref, gdown_ref, gkern_ref, ggain_ref, gbias_ref, gscale_ref,
    xpad, gpad, halo_x, halo_g, conv, scaled_ref, dconv, wout, upg, tok, dmx, hid, dpre,
    part_n, part_m, r1n, r1m, chip_n, chip_m, r2n, r2m, own_n, own_m,
    gpart, gsend, grecv, fsend, frecv, dscale, small, ar1, ar2, ar3,
    hx_s, hx_r, hg_s, hg_r, w_s, w_r, dm_s, dm_r, tk_s, tk_r,
    an_s, an_r, am_s, am_r, bn_s, bn_r, bm_s, bm_r,
    gz_s, gz_r, fi_s, fi_r, s1_s, s1_r, s2_s, s2_r, s3_s, s3_r,
):
    n_dp, n_sp, rows, cols, width, taps = sizes
    chips, share = n_dp // 2, n_dp // n_sp
    margin = taps // 2
    pixels = rows * cols
    hidden = wdown_ref.shape[0]
    d, s = lax.axis_index("dp"), lax.axis_index("space")
    chip, core = d // 2, lax.rem(d, 2)
    sibling = chip * 2 + (1 - core)
    home = d // share
    place = lax.rem(d, share)
    inside = (home == s).astype(jnp.int32)

    def is_self(b):
        return jnp.logical_and(home == s, place == b)

    def dp_peer(off):
        return lax.rem(d + off, n_dp)

    def sp_peer(off):
        return lax.rem(s + off, n_sp)

    barrier = pltpu.get_barrier_semaphore()

    def greet(device):
        pl.semaphore_signal(barrier, inc=1, device_id=device, device_id_type=pl.DeviceIdType.MESH)

    for off in range(1, n_dp):
        greet((dp_peer(off), s))
    for off in range(1, n_sp):
        greet((d, sp_peer(off)))
    for b in range(share):
        @pl.when(jnp.logical_not(is_self(b)))
        def _():
            greet((s * share + b, home))

    dmx[d] = (scale_ref[...] * cot_ref[...].astype(F32)).astype(BF16)
    for t in range(n_dp):
        wout[t] = wup_ref[:, t * hidden:(t + 1) * hidden]
    upg[d] = wout[d]
    for padded in (xpad, gpad):
        padded[...] = jnp.zeros(padded.shape, F32)
    xpad[margin:margin + rows, EDGE:EDGE + cols] = x_ref[...].astype(F32)
    dscale[...] = jnp.zeros(dscale.shape, F32)
    small[...] = jnp.zeros(small.shape, F32)
    pl.semaphore_wait(barrier, (n_dp - 1) + (n_sp - 1) + share - inside)

    has_up, has_down = s > 0, s < n_sp - 1

    def halo_copies(source, halo, send, recv):
        down = remote(source.at[pl.ds(rows - margin, margin)], halo.at[0], send.at[0], recv.at[0], (d, jnp.minimum(s + 1, n_sp - 1)))
        up = remote(source.at[pl.ds(0, margin)], halo.at[1], send.at[1], recv.at[1], (d, jnp.maximum(s - 1, 0)))
        return down, up

    def halo_start(copies):
        pl.when(has_down)(copies[0].start)
        pl.when(has_up)(copies[1].start)

    def halo_land(copies, halo, padded):
        @pl.when(has_up)
        def _():
            copies[0].wait_recv()
            padded[0:margin, EDGE:EDGE + cols] = halo[0].astype(F32)

        @pl.when(has_down)
        def _():
            copies[1].wait_recv()
            padded[rows + margin:, EDGE:EDGE + cols] = halo[1].astype(F32)

    def halo_sent(copies):
        pl.when(has_down)(copies[0].wait_send)
        pl.when(has_up)(copies[1].wait_send)

    hx = halo_copies(x_ref, halo_x, hx_s, hx_r)
    halo_start(hx)

    def spread(buf, send, recv):
        first = [remote(buf.at[d], buf.at[d], send.at[0], recv.at[d], (sibling, s))]
        for off in range(1, chips):
            first.append(remote(buf.at[d], buf.at[d], send.at[off], recv.at[d], (lax.rem(chip + off, chips) * 2 + core, s)))
        passed = []
        for off in range(1, chips):
            slot = lax.rem(chip + chips - off, chips) * 2 + core
            passed.append(remote(buf.at[slot], buf.at[slot], send.at[chips - 1 + off], recv.at[slot], (sibling, s)))
        last = []
        for off in range(chips):
            slot = lax.rem(chip + chips - off, chips) * 2 + (1 - core)
            last.append(remote(buf.at[slot], buf.at[slot], send.at[0], recv.at[slot], (sibling, s)))
        return first, passed, last

    dm_first, dm_passed, dm_last = spread(dmx, dm_s, dm_r)
    w_out = [remote(wout.at[dp_peer(off)], upg.at[d], w_s.at[off], w_r.at[d], (dp_peer(off), s)) for off in range(1, n_dp)]
    w_in = [remote(wout.at[dp_peer(off)], upg.at[dp_peer(off)], w_s.at[off], w_r.at[dp_peer(off)], (sibling, s)) for off in range(1, n_dp)]
    for copy in w_out:
        copy.start()
    for copy in dm_first:
        copy.start()

    halo_land(hx, halo_x, xpad)

    def convolve(padded, flip, lanes):
        total = jnp.zeros((rows, cols, LANES), F32)
        for b in range(taps):
            first = EDGE - margin + b
            window = padded[:, first:first + cols, lanes]
            for a in range(taps):
                at = (taps - 1 - a, taps - 1 - b) if flip else (a, b)
                tap = kern_ref[at[0], at[1]:at[1] + 1, lanes].reshape(1, 1, LANES)
                total = total + tap * window[a:a + rows]
        return total

    def lanes_of(c):
        return pl.ds(pl.multiple_of(c * LANES, LANES), LANES)

    @pl.loop(0, width // LANES)
    def _(c):
        conv[:, lanes_of(c)] = convolve(xpad, False, lanes_of(c)).reshape(pixels, LANES)

    center = conv[...]
    center = center - jnp.mean(center, axis=-1, keepdims=True)
    inverse = lax.rsqrt(jnp.mean(center * center, axis=-1, keepdims=True) + 1e-06)
    normal = center * inverse
    scaled_ref[...] = normal
    tok[d] = (normal * gain_ref[...] + bias_ref[...]).astype(BF16)

    tk_first, tk_passed, tk_last = spread(tok, tk_s, tk_r)
    for copy in tk_first:
        copy.start()
    for group in (dm_passed, tk_passed):
        for copy in group:
            copy.wait_recv()
            copy.start()
    for copy in w_in:
        copy.wait_recv()
    for group in (dm_last, tk_last):
        for copy in group:
            copy.wait_recv()

    def nn(a, b):
        return lax.dot_general(a, b, (((1,), (0,)), ((), ())), preferred_element_type=F32)

    def nt(a, b):
        return lax.dot_general(a, b, (((1,), (1,)), ((), ())), preferred_element_type=F32)

    def tn(a, b):
        return lax.dot_general(a, b, (((0,), (0,)), ((), ())), preferred_element_type=F32)

    def cross(kind, to):
        buf, got, send, recv = kind
        return remote(buf.at[to], got.at[to], send.at[to], recv.at[to], (sibling, s))

    def home_copy(kind, to):
        buf, got, send, recv = kind
        return remote(buf.at[to], got.at[chip], send.at[to], recv.at[chip], (to * 2 + core, s))

    cross_n, cross_m = (part_n, r1n, an_s, an_r), (part_m, r1m, am_s, am_r)
    home_n, home_m = (chip_n, r2n, bn_s, bn_r), (chip_m, r2m, bm_s, bm_r)

    def products(slot):
        up = upg[...].reshape(width, hidden)
        activation, slope = gelu_pair(nn(tok[slot], up))
        act = activation.astype(BF16)
        grad = (nt(dmx[slot], wdown_ref[...]) * slope).astype(BF16)
        hid[slot] = act
        dpre[slot] = grad
        mixed = nn(act, wdown_ref[...])
        dscale[...] += jnp.sum(dmx[slot].astype(F32) * mixed, axis=0, keepdims=True)
        return nt(grad, up), mixed

    @pl.loop(0, chips)
    def _(i):
        to = lax.rem(chip + 1 + i, chips)
        normed, mixed = products(to * 2 + (1 - core))
        part_n[to] = normed.astype(BF16)
        cross(cross_n, to).start()
        part_m[to] = mixed.astype(BF16)
        cross(cross_m, to).start()

    @pl.loop(0, chips - 1)
    def _(i):
        to = lax.rem(chip + 1 + i, chips)
        normed, mixed = products(to * 2 + core)
        cross(cross_n, to).wait_recv()
        chip_n[to] = (normed + r1n[to].astype(F32)).astype(BF16)
        home_copy(home_n, to).start()
        cross(cross_m, to).wait_recv()
        chip_m[to] = (mixed + r1m[to].astype(F32)).astype(BF16)

    normed, mixed = products(d)
    cross(cross_n, chip).wait_recv()
    own_n[...] = normed + r1n[chip].astype(F32)
    cross(cross_m, chip).wait_recv()
    own_m[...] = mixed + r1m[chip].astype(F32)

    strip = width // n_sp
    part_rows = strip // share
    flat = (n_dp * pixels,)

    def plane_copy(which, off, landing):
        to = sp_peer(off)
        slot = to if landing else s
        return remote(gsend.at[which, to], grecv.at[which, slot], gz_s.at[which, off], gz_r.at[which, slot], (d, to))

    for which, (left, right) in enumerate(((tok, dpre), (dmx, hid))):
        gpart[which] = tn(left[...].reshape(flat + (width,)), right[...].reshape(flat + (hidden,)))
        for k in range(n_sp):
            gsend[which, k] = gpart[which, k * strip:(k + 1) * strip].astype(BF16)
        for off in range(1, n_sp):
            plane_copy(which, off, False).start()

    def arrive(got, send, recv, own):
        total = own[...]
        for off in range(1, chips):
            source = lax.rem(chip + off, chips)
            remote(got.at[source], got.at[source], send.at[source], recv.at[source], (sibling, s)).wait_recv()
            total = total + got[source].astype(F32)
        return total

    d_norm = arrive(r2n, bn_s, bn_r, own_n)
    for off in range(1, chips):
        home_copy(home_m, lax.rem(chip + off, chips)).start()
    normal = scaled_ref[...]
    d_hat = d_norm * gain_ref[...]
    lead = jnp.mean(d_hat, axis=-1, keepdims=True)
    second = jnp.mean(d_hat * normal, axis=-1, keepdims=True)
    dconv[...] = (inverse * (d_hat - lead - normal * second)).astype(BF16).reshape(rows, cols, width)
    hg = halo_copies(dconv, halo_g, hg_s, hg_r)
    halo_start(hg)
    gpad[margin:margin + rows, EDGE:EDGE + cols] = dconv[...].astype(F32)

    per = small.shape[1]
    count = taps * taps

    def put(row, lanes, value):
        small[row // per, row % per:row % per + 1, lanes] = value

    everything = slice(None)
    put(count, everything, jnp.sum(d_norm * normal, axis=0, keepdims=True))
    put(count + 1, everything, jnp.sum(d_norm, axis=0, keepdims=True))
    put(count + 2, everything, dscale[...] / scale_ref[...])

    @pl.loop(0, width // LANES)
    def _(c):
        lanes = lanes_of(c)
        upstream = gpad[margin:margin + rows, EDGE:EDGE + cols, lanes]
        for b in range(taps):
            first = EDGE - margin + b
            window = xpad[:, first:first + cols, lanes]
            for a in range(taps):
                product = jnp.sum(window[a:a + rows] * upstream, axis=0)
                put(a * taps + b, lanes, jnp.sum(product, axis=0, keepdims=True))

    s1_out = [remote(small.at[dp_peer(off)], ar1.at[d], s1_s.at[off], s1_r.at[d], (dp_peer(off), s)) for off in range(1, n_dp)]
    s1_in = [remote(small.at[dp_peer(off)], ar1.at[dp_peer(off)], s1_s.at[off], s1_r.at[dp_peer(off)], (sibling, s)) for off in range(1, n_dp)]
    for copy in s1_out:
        copy.start()
    ar1[d] = small[d]

    halo_land(hg, halo_g, gpad)

    @pl.loop(0, width // LANES)
    def _(c):
        lanes = lanes_of(c)
        cot = cot_ref[:, lanes].astype(F32).reshape(rows, cols, LANES)
        dfeat_ref[:, :, lanes] = cot + convolve(gpad, True, lanes)

    for copy in s1_in:
        copy.wait_recv()
    ar2[s] = jnp.sum(ar1[...], axis=0)
    s2_out = [remote(ar2.at[s], ar2.at[s], s2_s.at[off], s2_r.at[s], (d, sp_peer(off))) for off in range(1, n_sp)]
    s2_in = [remote(ar2.at[s], ar2.at[sp_peer(off)], s2_s.at[off], s2_r.at[sp_peer(off)], (d, sp_peer(off))) for off in range(1, n_sp)]
    for copy in s2_out:
        copy.start()

    def owner_copy(which, b):
        return remote(fsend.at[which, b], frecv.at[which, place], fi_s.at[which, b], fi_r.at[which, place], (s * share + b, home))

    for which in range(2):
        total = gpart[which, pl.ds(pl.multiple_of(s * strip, strip), strip)]
        for off in range(1, n_sp):
            plane_copy(which, off, True).wait_recv()
            total = total + grecv[which, sp_peer(off)].astype(F32)
        for b in range(share):
            fsend[which, b] = total[b * part_rows:(b + 1) * part_rows].astype(BF16)
            pl.when(jnp.logical_not(is_self(b)))(owner_copy(which, b).start)

            @pl.when(is_self(b))
            def _():
                frecv[which, b] = fsend[which, b]

    mixed = arrive(r2m, bm_s, bm_r, own_m)
    res_ref[...] = (x_ref[...].reshape(pixels, width).astype(F32) + scale_ref[...] * mixed).astype(BF16).reshape(rows, cols, width)

    for copy in s2_in:
        copy.wait_recv()
    ar3[d] = jnp.sum(ar2[...], axis=0)
    s3_out = [remote(ar3.at[d], ar3.at[d], s3_s.at[off], s3_r.at[d], (dp_peer(off), s)) for off in range(1, n_dp)]
    s3_in = [remote(ar3.at[d], ar3.at[dp_peer(off)], s3_s.at[off], s3_r.at[dp_peer(off)], (sibling, s)) for off in range(1, n_dp)]
    for copy in s3_out:
        copy.start()

    for which, out in enumerate((gup_ref, gdown_ref)):
        for b in range(share):
            landed = remote(fsend.at[which, b], frecv.at[which, b], fi_s.at[which, b], fi_r.at[which, b], (sibling, s))
            pl.when(jnp.logical_not(is_self(b)))(landed.wait_recv)
        for b in range(share):
            out[:, b * hidden:(b + 1) * hidden] = frecv[which, b].astype(F32)

    for copy in s3_in:
        copy.wait_recv()

    def take(row):
        return ar3[row // per, row % per:row % per + 1]

    for a in range(taps):
        for b in range(taps):
            gkern_ref[a, b:b + 1] = take(a * taps + b)
    ggain_ref[...] = take(count)
    gbias_ref[...] = take(count + 1)
    gscale_ref[...] = take(count + 2)

    halo_sent(hx)
    halo_sent(hg)
    for group in (w_out, dm_first, dm_passed, tk_first, tk_passed, s1_out, s2_out, s3_out):
        for copy in group:
            copy.wait_send()
    for which in range(2):
        for off in range(1, n_sp):
            plane_copy(which, off, False).wait_send()
        for b in range(share):
            pl.when(jnp.logical_not(is_self(b)))(owner_copy(which, b).wait_send)

    for off in range(chips):
        to = lax.rem(chip + 1 + off, chips)
        cross(cross_n, to).wait_send()
        cross(cross_m, to).wait_send()
        if off < chips - 1:
            home_copy(home_n, to).wait_send()
            home_copy(home_m, to).wait_send()


def local(features, cotangent, dw_kernel, ln_gain, ln_bias, layer_scale, w_up, w_down):
    n_dp, n_sp = lax.axis_size("dp"), lax.axis_size("space")
    _, rows, cols, width = features.shape
    taps = dw_kernel.shape[0]
    margin = taps // 2
    pixels = rows * cols
    hidden = w_down.shape[0]
    chips, share = n_dp // 2, n_dp // n_sp
    strip = width // n_sp
    part_rows = strip // share
    count = taps * taps
    per = -(-(count + 3) // n_dp)
    blocks = (n_dp, w_up.shape[0], hidden)
    padded = (rows + 2 * margin, cols + 2 * EDGE, width)
    dma = lambda k: pltpu.SemaphoreType.DMA((k,))
    vm = pltpu.VMEM
    scratch = [
        vm(padded, F32), vm(padded, F32),
        vm((2, margin, cols, width), BF16), vm((2, margin, cols, width), BF16),
        vm((pixels, width), F32), vm((pixels, width), F32), vm((rows, cols, width), BF16),
        vm(blocks, BF16), vm(blocks, BF16),
        vm((n_dp, pixels, width), BF16), vm((n_dp, pixels, width), BF16),
        vm((n_dp, pixels, hidden), BF16), vm((n_dp, pixels, hidden), BF16),
    ]
    scratch += [vm((chips, pixels, width), BF16)] * 8
    scratch += [vm((pixels, width), F32)] * 2
    scratch += [
        vm((2, width, hidden), F32),
        vm((2, n_sp, strip, hidden), BF16), vm((2, n_sp, strip, hidden), BF16),
        vm((2, share, part_rows, hidden), BF16), vm((2, share, part_rows, hidden), BF16),
        vm((1, width), F32),
        vm((n_dp, per, width), F32), vm((n_dp, per, width), F32),
        vm((n_sp, per, width), F32), vm((n_dp, per, width), F32),
    ]
    scratch += [dma(2)] * 4 + [dma(n_dp)] * 6 + [dma(chips)] * 8
    pair = lambda k: pltpu.SemaphoreType.DMA((2, k))
    scratch += [pair(n_sp)] * 2 + [pair(share)] * 2 + [dma(n_dp)] * 2 + [dma(n_sp)] * 2 + [dma(n_dp)] * 2
    whole = pl.BlockSpec(memory_space=pltpu.VMEM)
    result, d_feat, grad_up, grad_down, kernel_sum, gain_sum, bias_sum, scale_sum = pl.pallas_call(
        functools.partial(block_kernel, (n_dp, n_sp, rows, cols, width, taps)),
        out_shape=(
            jax.ShapeDtypeStruct((rows, cols, width), BF16),
            jax.ShapeDtypeStruct((rows, cols, width), F32),
            jax.ShapeDtypeStruct((part_rows, share * hidden), F32),
            jax.ShapeDtypeStruct((part_rows, share * hidden), F32),
            jax.ShapeDtypeStruct((taps, taps, width), F32),
        )
        + (jax.ShapeDtypeStruct((1, width), F32),) * 3,
        in_specs=[whole] * 8,
        out_specs=(whole,) * 8,
        scratch_shapes=scratch,
        compiler_params=pltpu.CompilerParams(
            collective_id=0, has_side_effects=True, vmem_limit_bytes=60 << 20
        ),
    )(
        features[0],
        cotangent[0].reshape(pixels, width),
        dw_kernel,
        ln_gain.reshape(1, width),
        ln_bias.reshape(1, width),
        layer_scale.reshape(1, width),
        w_up,
        w_down,
    )
    regions = float(n_dp)
    return (
        result[None],
        d_feat[None],
        grad_up / regions,
        grad_down.T / regions,
        kernel_sum / regions,
        gain_sum[0] / regions,
        bias_sum[0] / regions,
        scale_sum[0] / regions,
    )


def solution(mesh):
    in_specs = (
        P("dp", "space", None, None),
        P("dp", "space", None, None),
        P(),
        P(),
        P(),
        P(),
        P("dp", None),
        P("dp", None),
    )
    out_specs = (
        P("dp", "space", None, None),
        P("dp", "space", None, None),
        P("dp", "space"),
        P("space", "dp"),
        P(),
        P(),
        P(),
        P(),
    )
    return jax.shard_map(local, mesh=mesh, in_specs=in_specs, out_specs=out_specs, check_vma=False)
```
